32 devices in a mesh: wide: 8 (over y, x, core), narrow: 4 (over z).
Axes of the slice: x: 2, y: 2, z: 4, core: 2. Of those that a mesh axis runs over, the one named last changes fastest.
Arguments:
- divergence: float32 [64, 32, 512], P('wide', None, 'narrow'), may hold values from -6 to 6
- pressure_start: float32 [64, 32, 512], P('wide', None, 'narrow'), may hold values from -3 to 3
- phase: int32 [64, 32, 512], P('wide', None, 'narrow'), may hold values 0 or 1
- velocity_cot: float32 [3, 64, 32, 512], P(None, 'wide', None, 'narrow'), may hold values from -6 to 6
Outputs:
- grad_divergence: float32 [64, 32, 512], P('wide', None, 'narrow')
- grad_pressure: float32 [64, 32, 512], P('wide', None, 'narrow')
- grad_faces: float32 [3, 64, 32, 512], P(None, 'wide', None, 'narrow')
The draws below stay inside these ranges and needn't reach their ends.
Inputs may be any that keep to these rules, and one draw needn't show every extreme that they name: `phase`: 0 marks a liquid cell, 1 a gas cell.
All inputs are finite; a program needn't handle non-finite values. No bound on the sum of `phase` on one device may be relied on, other than what follows from the above.
Results may differ from the reference program's by a relative error of at most 0.0003.
Values sent between devices are 32-bit elements; how exact they have to be, the bound alone decides.
No kernel may reach another device: no remote copies, remote signals or barrier semaphores. Data moves between devices by JAX's collectives and lax.ppermute only.
A program may use at most 64 MiB of HBM per device.

```python
import math
import jax
import jax.numpy as jnp
from jax import lax

NY = 32
SWEEPS = 6
NX = 64
NZ = 512


def touch_ends(values, key, low, high):
    longest = values.shape.index(max(values.shape))
    spots = []
    for shift in (0, 1):
        where = [jax.random.randint(jax.random.fold_in(key, axis), (), 0, length) for axis, length in enumerate(values.shape)]
        where[longest] = (where[longest] + shift) % values.shape[longest]
        spots.append(tuple(where))
    return values.at[spots[0]].set(low).at[spots[1]].set(high)


def levels(key, extent, shards, low, high):
    level, own = 1.0, jax.random.fold_in(key, 6)
    for axis_at, shards_of in shards:
        draws = jnp.exp(jax.random.uniform(jax.random.fold_in(own, axis_at), (shards_of,), jnp.float32, low / len(shards), high / len(shards)))
        level = level * jnp.repeat(draws, extent[axis_at] // shards_of).reshape([-1 if axis == axis_at else 1 for axis in range(len(extent))])
    return level


def gaussian(rng, shape, width, most, split=(), held_as=jnp.bfloat16):
    level = levels(rng, shape, split, -0.22, 0.18) if split else 1.0
    drawn = jax.random.normal(rng, shape, jnp.float32) * width * level
    return jnp.minimum(jnp.maximum(drawn, -most), most).astype(held_as)


def setup_inputs(seed: int = 0) -> dict:
    key_of = jax.random.split(jax.random.key(seed), 5)
    divergence = gaussian(key_of[0], (NX, NY, NZ), 1.0, 6.0, ((0, 8), (2, 4)), jnp.float32)
    pressure_start = gaussian(key_of[1], (NX, NY, NZ), 0.5, 3.0, ((0, 8), (2, 4)), jnp.float32)
    phase = touch_ends((jax.random.randint(key_of[2], (NX, NY, NZ), 0, 3) < 1).astype(jnp.int32), jax.random.fold_in(key_of[2], 1), 0, 1)
    velocity_cot = gaussian(key_of[3], (3, NX, NY, NZ), 1.0, 6.0, ((1, 8), (3, 4)), jnp.float32)
    return {"divergence": divergence, "pressure_start": pressure_start, "phase": phase, "velocity_cot": velocity_cot}


gas_density = 0.25
lower_bound = 0.25
upper_bound = 2.0

def chebyshev_weights(count):
    center = 0.5 * (upper_bound + lower_bound)
    radius = 0.5 * (upper_bound - lower_bound)
    roots = [center + radius * math.cos(math.pi * (2 * number + 1) / (2 * count)) for number in range(count)]
    order = []
    for number in range(count // 2):
        order.append(number)
        order.append(count - 1 - number)
    if count % 2 == 1:
        order.append(count // 2)
    return [1.0 / roots[position] for position in order]

def shift_up(array, axis_dim):
    length = array.shape[axis_dim]
    zeros = jnp.zeros_like(lax.slice_in_dim(array, 0, 1, axis=axis_dim))
    return jnp.concatenate([lax.slice_in_dim(array, 1, length, axis=axis_dim), zeros], axis=axis_dim)

def shift_down(array, axis_dim):
    length = array.shape[axis_dim]
    zeros = jnp.zeros_like(lax.slice_in_dim(array, 0, 1, axis=axis_dim))
    return jnp.concatenate([zeros, lax.slice_in_dim(array, 0, length - 1, axis=axis_dim)], axis=axis_dim)

def reference(divergence, pressure_start, phase, velocity_cot):
    density = jnp.where(phase == 1, gas_density, 1.0).astype(jnp.float32)
    upper = []
    edges = []
    for axis_dim in range(3):
        above = shift_up(density, axis_dim)
        upper.append(2.0 / (density + jnp.where(above > 0.0, above, density)))
        below = shift_down(density, axis_dim)
        edges.append(jnp.where(below > 0.0, 0.0, 1.0 / density).astype(jnp.float32))
    weights = chebyshev_weights(SWEEPS)

    def make_sweep(weight):

        def sweep(pressure, source, faces):
            lower = [shift_down(faces[axis_dim], axis_dim) + edges[axis_dim] for axis_dim in range(3)]
            diag = faces[0] + lower[0] + faces[1] + lower[1] + faces[2] + lower[2]
            applied = jnp.zeros_like(pressure)
            for axis_dim in range(3):
                applied = applied + faces[axis_dim] * (pressure - shift_up(pressure, axis_dim))
                applied = applied + lower[axis_dim] * (pressure - shift_down(pressure, axis_dim))
            return pressure + weight * (source - applied) / diag
        return jax.checkpoint(sweep)

    def forward(source, start, faces):
        pressure = start
        for weight in weights:
            pressure = make_sweep(weight)(pressure, source, faces)
        return jnp.stack([-faces[axis_dim] * (shift_up(pressure, axis_dim) - pressure) for axis_dim in range(3)])
    result, pullback = jax.vjp(forward, divergence, pressure_start, tuple(upper))
    grad_source, grad_start, grad_upper = pullback(velocity_cot)
    return (grad_source, grad_start, jnp.stack(list(grad_upper)))
```

```python
import math

import jax
import jax.numpy as jnp
from jax import lax
from jax.experimental import pallas as pl
from jax.experimental.pallas import tpu as pltpu
from jax.sharding import PartitionSpec as P

SWEEPS = 6

gas_density = 0.25
lower_bound = 0.25
upper_bound = 2.0

FACE = (1.0, 2.0 / (1.0 + gas_density), 1.0 / gas_density)


def chebyshev_weights(count):
    center = 0.5 * (upper_bound + lower_bound)
    radius = 0.5 * (upper_bound - lower_bound)
    roots = [
        center + radius * math.cos(math.pi * (2 * number + 1) / (2 * count))
        for number in range(count)
    ]
    order = []
    for number in range(count // 2):
        order.append(number)
        order.append(count - 1 - number)
    return [1.0 / roots[position] for position in order]


def face(pair):
    return jnp.where(pair < 0.5, FACE[0], jnp.where(pair < 1.5, FACE[1], FACE[2]))


def iota(dim):
    return lax.broadcasted_iota(jnp.int32, (32, 128), dim)


def y_up(v):
    return pltpu.roll(v, v.shape[0] - 1, 0)


def y_down(v):
    return pltpu.roll(v, 1, 0)


def z_up(v):
    return pltpu.roll(v, v.shape[1] - 1, 1)


def z_down(v):
    return pltpu.roll(v, 1, 1)


HALO = SWEEPS + 1
PLANES = 2 * HALO + 2 * SWEEPS
ROWS = 32
CORNER = 2 * ROWS + 8


def pack_kernel(where_ref, ph_ref, dv_ref, p_ref, vc_ref, xa_ref, xb_ref, za_ref, zb_ref, row_ref, adj_ref, up_ref, down_ref):
    cells_x = ph_ref.shape[0]
    x_even = where_ref[0] % 2 == 0
    z_even = where_ref[2] % 2 == 0
    lane = iota(1)
    row = iota(0)
    before = None
    for i in range(cells_x):
        ph = ph_ref[i].astype(jnp.float32)
        adj = jnp.zeros_like(ph)
        if before is not None:
            adj = adj - before
        if i + 1 < cells_x:
            before = face(ph + ph_ref[i + 1].astype(jnp.float32)) * vc_ref[0, i]
            adj = adj + before
        flux = face(ph + jnp.where(row == ph.shape[0] - 1, ph, y_up(ph))) * vc_ref[1, i]
        adj = adj + flux - jnp.where(row == 0, 0.0, y_down(flux))
        flux = jnp.where(lane == ph.shape[1] - 1, 0.0, face(ph + z_up(ph)) * vc_ref[2, i])
        adj = adj + flux - z_down(flux)
        adj_ref[i] = adj

    first = cells_x - HALO
    n = SWEEPS

    def upward(out):
        out[0:HALO] = ph_ref[first:].astype(jnp.float32)
        out[HALO : HALO + n] = dv_ref[first + 1 :]
        out[HALO + n : HALO + 2 * n] = adj_ref[first + 1 :]
        out[HALO + 2 * n : HALO + 3 * n] = p_ref[first + 1 :]
        out[HALO + 3 * n] = vc_ref[0, cells_x - 1]

    def downward(out):
        out[0:HALO] = ph_ref[0:HALO].astype(jnp.float32)
        out[HALO : HALO + n] = dv_ref[0:n]
        out[HALO + n : HALO + 2 * n] = adj_ref[0:n]
        out[HALO + 2 * n : 2 * HALO + 2 * n] = p_ref[0:HALO]

    @pl.when(x_even)
    def _():
        upward(xa_ref)
        downward(xb_ref)

    @pl.when(jnp.logical_not(x_even))
    def _():
        upward(xb_ref)
        downward(xa_ref)

    cells = cells_x * ph_ref.shape[1]
    width = ph_ref.shape[2]

    def turned(v):
        return v.reshape(cells, width).T

    t = turned(ph_ref[...].astype(jnp.float32))
    up_ref[0:HALO] = t[width - HALO :]
    down_ref[0:HALO] = t[0:HALO]
    t = turned(dv_ref[...])
    up_ref[HALO : HALO + n] = t[width - n :]
    down_ref[HALO : HALO + n] = t[0:n]
    t = turned(adj_ref[...])
    up_ref[HALO + n : HALO + 2 * n] = t[width - n :]
    down_ref[HALO + n : HALO + 2 * n] = t[0:n]
    t = turned(p_ref[...])
    up_ref[HALO + 2 * n : HALO + 3 * n] = t[width - n :]
    down_ref[HALO + 2 * n : 2 * HALO + 2 * n] = t[0:HALO]
    t = turned(vc_ref[2])
    up_ref[HALO + 3 * n : HALO + 3 * n + 1] = t[width - 1 :]
    row_ref[...] = t[width - 8 :]
    t = turned(vc_ref[0])
    up_ref[2 * HALO + 2 * n + 0 : 2 * HALO + 3 * n] = t[width - n :]
    down_ref[2 * HALO + 2 * n : 2 * HALO + 3 * n] = t[0:n]

    @pl.when(z_even)
    def _():
        za_ref[...] = up_ref[...]
        zb_ref[...] = down_ref[...]

    @pl.when(jnp.logical_not(z_even))
    def _():
        zb_ref[...] = up_ref[...]
        za_ref[...] = down_ref[...]


def unpack_kernel(where_ref, own_ref, ca_ref, cb_ref, h_ref, v_ref, e_ref, t_ref):
    x_even = where_ref[0] % 2 == 0
    z_even = where_ref[2] % 2 == 0
    n = SWEEPS
    width = t_ref.shape[1]
    cells = own_ref.shape[1]
    t_ref[...] = jnp.zeros_like(t_ref)
    for block in range(3):
        if block == 1:
            part = own_ref[...]
        else:
            low_is_a = jnp.logical_not(x_even) if block == 0 else x_even
            part = jnp.where(low_is_a, ca_ref[...], cb_ref[...])
        zl = jnp.where(z_even, part[ROWS : 2 * ROWS], part[0:ROWS])
        zh = jnp.where(z_even, part[0:ROWS], part[ROWS : 2 * ROWS])
        at = slice(block * cells, (block + 1) * cells)
        t_ref[0, 0:HALO, at] = zh[0:HALO]
        t_ref[0, width - HALO :, at] = zl[0:HALO]
        for field in (1, 2):
            first = HALO + (field - 1) * n
            t_ref[field, 0:n, at] = zh[first : first + n]
            t_ref[field, width - n :, at] = zl[first : first + n]
        first = HALO + 2 * n
        t_ref[3, 0:HALO, at] = zh[first : first + HALO]
        t_ref[3, width - n :, at] = zl[first : first + n]
        t_ref[4, width - 1 :, at] = zl[first + n : first + n + 1]
        t_ref[4, width // 2 - 1 : width // 2, at] = part[2 * ROWS + 7 : 2 * ROWS + 8]
        t_ref[5, 0:n, at] = zh[2 * HALO + 2 * n :]
        t_ref[5, width - n :, at] = zl[2 * HALO + 2 * n :]
    planes = h_ref.shape[1]
    for field in range(4):
        h_ref[field] = t_ref[field].T.reshape(planes, cells * 3 // planes, width)
    v_ref[...] = t_ref[4].T.reshape(planes, cells * 3 // planes, width)
    third = planes // 3
    own = t_ref[5].T.reshape(planes, cells * 3 // planes, width)
    e_ref[0] = own[third - 1]
    e_ref[1] = own[2 * third - 1]


def main_kernel(
    where_ref, ph_ref, dv_ref, p_ref, vc_ref, adj_ref, xa_ref, xb_ref, h_ref, v_ref, e_ref,
    gd_ref, gp_ref, gf_ref,
    e1, e2, f0_ref, c_ref, s_ref, ps, us, diag_ref, r_ref,
):
    cells_x, ny, width = ph_ref.shape
    n = SWEEPS
    off = cells_x
    wi = where_ref[0]
    x_first = wi == 0
    x_last = wi == where_ref[1] - 1
    z_first = where_ref[2] == 0
    z_last = where_ref[2] == where_ref[3] - 1
    x_even = wi % 2 == 0
    lane = iota(1)
    row = iota(0)
    lane0 = lane == 0
    lane_end = lane == width - 1
    weights = chebyshev_weights(SWEEPS)

    def low(k):
        return jnp.where(x_even, xb_ref[k], xa_ref[k])

    def high(k):
        return jnp.where(x_even, xa_ref[k], xb_ref[k])

    for i in range(cells_x):
        e1[i + off] = ph_ref[i].astype(jnp.float32)
    for k in range(HALO):
        e1[off - HALO + k] = low(k)
        e1[off + cells_x + k] = high(k)
    e1[off - 1] = jnp.where(x_first, e1[off], e1[off - 1])
    e1[off + cells_x] = jnp.where(x_last, e1[off + cells_x - 1], e1[off + cells_x])
    for i in range(-HALO, cells_x + HALO):
        e2[i + off] = h_ref[0, i + off]
    e2[off - 1] = jnp.where(x_first, e2[off], e2[off - 1])
    e2[off + cells_x] = jnp.where(x_last, e2[off + cells_x - 1], e2[off + cells_x])
    at_low = jnp.logical_and(lane_end, z_first)
    at_high = jnp.logical_and(lane0, z_last)
    for i in range(-HALO, cells_x + HALO):
        ph1 = e1[i + off]
        e2[i + off] = jnp.where(at_high, z_down(ph1), jnp.where(at_low, z_up(ph1), e2[i + off]))

    in_low = jnp.logical_not(x_first)
    in_high = jnp.logical_not(x_last)
    side_high = jnp.logical_and(lane <= HALO - 1, jnp.logical_not(z_last))
    side_low = jnp.logical_and(lane >= width - HALO, jnp.logical_not(z_first))
    side = jnp.logical_or(side_low, side_high)
    core = jnp.logical_and(
        side, jnp.logical_or(lane < HALO - 1, lane > width - HALO)
    )

    def within(i):
        return in_low if i < 0 else (in_high if i >= cells_x else None)

    def masked(i, col, value, cover):
        flag = within(i)
        if col == 0:
            return value if flag is None else jnp.where(flag, value, 0.0)
        return jnp.where(cover if flag is None else jnp.logical_and(cover, flag), value, 0.0)

    for i in range(-n, cells_x + HALO):
        if i < 0:
            value = low(HALO + 2 * n + n + i)
        elif i >= cells_x:
            value = high(HALO + 2 * n + i - cells_x)
        else:
            value = p_ref[i]
        ps[0, 0, i + off] = masked(i, 0, value, None)
        ps[0, 1, i + off] = masked(i, 1, h_ref[3, i + off], side)

    for i in range(-HALO, cells_x + n):
        f0_ref[0, i + off] = face(e1[i + off] + e1[i + 1 + off])
        f0_ref[1, i + off] = face(e2[i + off] + e2[i + 1 + off])

    cross = {}
    for number, i in enumerate((-1, cells_x - 1)):
        value = low(HALO + 3 * n) if i < 0 else vc_ref[0, i]
        flux = (f0_ref[0, i + off] * value, f0_ref[1, i + off] * e_ref[number])
        cross[i] = tuple(jnp.where(in_low, v, 0.0) for v in flux) if i < 0 else flux

    for i in range(-n, cells_x + n):
        j = i + off
        ph = (e1[j], e2[j])
        up_z = [z_up(v) for v in ph]
        f2 = [
            face(ph[0] + jnp.where(lane_end, up_z[1], up_z[0])),
            face(ph[1] + jnp.where(lane_end, up_z[0], up_z[1])),
        ]
        down_z = [z_down(v) for v in f2]
        l2 = [jnp.where(lane0, down_z[1], down_z[0]), jnp.where(lane0, down_z[0], down_z[1])]
        if 0 <= i < cells_x:
            last = vc_ref[2, i]
        else:
            last = pltpu.roll(v_ref[j], width // 2, 1)
        g = [
            jnp.where(lane_end, f2[0] * last, 0.0),
            jnp.where(jnp.logical_and(lane_end, jnp.logical_not(z_first)), f2[1] * v_ref[j], 0.0),
        ]
        down_g = [z_down(v) for v in g]
        for col in range(2):
            f1 = face(ph[col] + jnp.where(row == ny - 1, ph[col], y_up(ph[col])))
            l1 = face(ph[col] + jnp.where(row == 0, ph[col], y_down(ph[col])))
            f0 = f0_ref[col, j]
            l0 = f0_ref[col, j - 1]
            diag = f0 + l0 + f1 + l1 + f2[col] + l2[col]
            inv = masked(i, col, 1.0 / diag, core)
            if col == 0 and 0 <= i < cells_x:
                diag_ref[i] = diag
            c_ref[0, col, j] = f0 * inv
            c_ref[1, col, j] = l0 * inv
            c_ref[2, col, j] = jnp.where(row == ny - 1, 0.0, f1 * inv)
            c_ref[3, col, j] = jnp.where(row == 0, 0.0, l1 * inv)
            c_ref[4, col, j] = f2[col] * inv
            c_ref[5, col, j] = l2[col] * inv
            if col == 1:
                source = h_ref[1, j]
                adj = h_ref[2, j]
            elif i < 0:
                source = low(HALO + n + i)
                adj = low(HALO + n + n + i)
            elif i >= cells_x:
                source = high(HALO + i - cells_x)
                adj = high(HALO + n + i - cells_x)
            else:
                source = dv_ref[i]
                adj = adj_ref[i]
            if i in cross:
                adj = adj + cross[i][col]
            if i - 1 in cross:
                adj = adj - cross[i - 1][col]
            adj = adj + g[col] - down_g[1 - col]
            keep = masked(i, col, jnp.ones_like(inv), core) > 0.5
            s_ref[col, j] = jnp.where(keep, source, 0.0) * inv
            us[0, col, j] = jnp.where(keep, adj, 0.0) * inv

    def spread(state, k, col, j):
        v = (state[k, 0, j], state[k, 1, j])
        up = jnp.where(lane_end, z_up(v[1 - col]), z_up(v[col]))
        down = jnp.where(lane0, z_down(v[1 - col]), z_down(v[col]))
        total = c_ref[0, col, j] * state[k, col, j + 1] + c_ref[1, col, j] * state[k, col, j - 1]
        total = total + c_ref[2, col, j] * y_up(v[col]) + c_ref[3, col, j] * y_down(v[col])
        return total + c_ref[4, col, j] * up + c_ref[5, col, j] * down

    us[0, 0, off + cells_x + n] = jnp.zeros((ny, width), jnp.float32)
    us[0, 1, off + cells_x + n] = jnp.zeros((ny, width), jnp.float32)
    us[0, 0, off - n - 1] = jnp.zeros((ny, width), jnp.float32)
    us[0, 1, off - n - 1] = jnp.zeros((ny, width), jnp.float32)
    for k in range(n):
        w = weights[k]
        wu = weights[n - 1 - k]
        for i in range(-(n - 1) + k, cells_x + n - k):
            j = i + off
            for col in range(2):
                p = ps[k, col, j]
                ps[k + 1, col, j] = (1.0 - w) * p + w * (s_ref[col, j] + spread(ps, k, col, j))
                if i < cells_x + n - 1 - k:
                    u = us[k, col, j]
                    us[k + 1, col, j] = (1.0 - wu) * u + wu * spread(us, k, col, j)

    for i in range(cells_x + 1):
        j = i + off
        for col in range(2):
            total = jnp.zeros((ny, width), jnp.float32)
            for k in range(n):
                total = total + us[n - 1 - k, col, j] * (ps[k + 1, col, j] - ps[k, col, j])
            r_ref[col, j] = total
    for i in range(cells_x):
        j = i + off
        gp_ref[i] = us[n, 0, j] * diag_ref[i]
        gd = jnp.zeros((ny, width), jnp.float32)
        terms = [jnp.zeros((ny, width), jnp.float32) for _ in range(3)]

        def rises(v, x_next, v2):
            z_next = jnp.where(lane_end, z_up(v2), z_up(v))
            y_next = jnp.where(row == ny - 1, 0.0, y_up(v))
            return x_next - v, y_next - v, z_next - v

        for k in range(n):
            u = us[n - 1 - k, 0, j]
            gd = gd + weights[k] * u
            p = ps[k, 0, j]
            rise_u = rises(u, us[n - 1 - k, 0, j + 1], us[n - 1 - k, 1, j])
            rise_p = rises(p, ps[k, 0, j + 1], ps[k, 1, j])
            for a in range(3):
                terms[a] = terms[a] + weights[k] * (rise_u[a] * rise_p[a])
        gd_ref[i] = gd
        p = ps[n, 0, j]
        rise = rises(p, ps[n, 0, j + 1], ps[n, 1, j])
        r = r_ref[0, j]
        y_next = jnp.where(row == ny - 1, 0.0, y_up(r))
        z_next = jnp.where(lane_end, z_up(r_ref[1, j]), z_up(r))
        nexts = (r_ref[0, j + 1], y_next, z_next)
        for a in range(3):
            gf_ref[a, i] = -vc_ref[a, i] * rise[a] - terms[a] - (r + nexts[a])


def swaps(size, other, odd, spare_first):
    pairs = []
    for i in range(size):
        for k in range(other):
            partner = ((i + 1) ^ 1) - 1 if odd else i ^ 1
            target = (partner, k) if 0 <= partner < size else (i, k ^ 1)
            source = (i, k)
            pairs.append((source, target))
    return pairs


def flat_pairs(pairs, narrow, turned):
    def flat(at):
        return at[1] * narrow + at[0] if turned else at[0] * narrow + at[1]

    return [(flat(source), flat(target)) for source, target in pairs]


def per_device(divergence, pressure_start, phase, velocity_cot):
    cells_x, ny, cells_z = divergence.shape
    wide, narrow = lax.axis_size("wide"), lax.axis_size("narrow")
    axes = ("wide", "narrow")
    x_even = flat_pairs(swaps(wide, narrow, False, True), narrow, False)
    x_odd = flat_pairs(swaps(wide, narrow, True, True), narrow, False)
    z_even = flat_pairs(swaps(narrow, wide, False, True), narrow, True)
    z_odd = flat_pairs(swaps(narrow, wide, True, True), narrow, True)
    at = jnp.stack(
        [lax.axis_index("wide"), jnp.int32(wide), lax.axis_index("narrow"), jnp.int32(narrow)]
    ).astype(jnp.int32)

    f32 = jnp.float32
    smem = pl.BlockSpec(memory_space=pltpu.SMEM)
    vmem = pl.BlockSpec(memory_space=pltpu.VMEM)

    def shape(*dims):
        return jax.ShapeDtypeStruct(dims, f32)

    slots = 2 * HALO + 2 * SWEEPS
    cells = cells_x * ny
    xa, xb, za, zb, edge, adj = pl.pallas_call(
        pack_kernel,
        out_shape=(
            shape(slots, ny, cells_z), shape(slots, ny, cells_z), shape(ROWS, cells), shape(ROWS, cells),
            shape(8, cells), shape(cells_x, ny, cells_z),
        ),
        in_specs=[smem] + [vmem] * 4,
        out_specs=(vmem,) * 6,
        scratch_shapes=[pltpu.VMEM((ROWS, cells), f32)] * 2,
        name="pack",
    )(at, phase, divergence, pressure_start, velocity_cot)

    got_xb = lax.ppermute(xb, axes, x_odd)
    got_xa = lax.ppermute(xa, axes, x_even)
    got_za = lax.ppermute(za, axes, z_even)
    got_zb = lax.ppermute(zb, axes, z_odd)
    corner = jnp.concatenate([got_za, got_zb, edge], axis=0)
    got_cb = lax.ppermute(corner, axes, x_odd)
    got_ca = lax.ppermute(corner, axes, x_even)

    total = 3 * cells_x
    sides, flux_z, flux_x = pl.pallas_call(
        unpack_kernel,
        out_shape=(shape(4, total, ny, cells_z), shape(total, ny, cells_z), shape(2, ny, cells_z)),
        in_specs=[smem] + [vmem] * 3,
        out_specs=(vmem,) * 3,
        scratch_shapes=[pltpu.VMEM((6, cells_z, 3 * cells), f32)],
        name="unpack",
    )(at, corner, got_ca, got_cb)

    block = (total, ny, cells_z)
    return pl.pallas_call(
        main_kernel,
        out_shape=(
            shape(cells_x, ny, cells_z), shape(cells_x, ny, cells_z), shape(3, cells_x, ny, cells_z),
        ),
        in_specs=[smem] + [vmem] * 10,
        out_specs=(vmem,) * 3,
        scratch_shapes=[
            pltpu.VMEM(block, f32),
            pltpu.VMEM(block, f32),
            pltpu.VMEM((2, *block), f32),
            pltpu.VMEM((6, 2, *block), f32),
            pltpu.VMEM((2, *block), f32),
            pltpu.VMEM((SWEEPS + 1, 2, *block), f32),
            pltpu.VMEM((SWEEPS + 1, 2, *block), f32),
            pltpu.VMEM((cells_x, ny, cells_z), f32),
            pltpu.VMEM((2, *block), f32),
        ],
        name="sweeps",
    )(at, phase, divergence, pressure_start, velocity_cot, adj, got_xa, got_xb, sides, flux_z, flux_x)


def solution(mesh):
    in_specs = (
        P("wide", None, "narrow"),
        P("wide", None, "narrow"),
        P("wide", None, "narrow"),
        P(None, "wide", None, "narrow"),
    )
    out_specs = (
        P("wide", None, "narrow"),
        P("wide", None, "narrow"),
        P(None, "wide", None, "narrow"),
    )
    return jax.shard_map(
        per_device, mesh=mesh, in_specs=in_specs, out_specs=out_specs, check_vma=False
    )
```

```python
import math

import jax
import jax.numpy as jnp
from jax import lax
from jax.experimental import pallas as pl
from jax.experimental.pallas import tpu as pltpu
from jax.sharding import PartitionSpec as P

SWEEPS = 6

gas_density = 0.25
lower_bound = 0.25
upper_bound = 2.0

FACE = (1.0, 2.0 / (1.0 + gas_density), 1.0 / gas_density)


def chebyshev_weights(count):
    center = 0.5 * (upper_bound + lower_bound)
    radius = 0.5 * (upper_bound - lower_bound)
    roots = [
        center + radius * math.cos(math.pi * (2 * number + 1) / (2 * count))
        for number in range(count)
    ]
    order = []
    for number in range(count // 2):
        order.append(number)
        order.append(count - 1 - number)
    return [1.0 / roots[position] for position in order]


def face(pair):
    return jnp.where(pair < 0.5, FACE[0], jnp.where(pair < 1.5, FACE[1], FACE[2]))


def iota(dim):
    return lax.broadcasted_iota(jnp.int32, (32, 128), dim)


def y_up(v):
    return pltpu.roll(v, v.shape[0] - 1, 0)


def y_down(v):
    return pltpu.roll(v, 1, 0)


def z_up(v):
    return pltpu.roll(v, v.shape[1] - 1, 1)


def z_down(v):
    return pltpu.roll(v, 1, 1)


HALO = SWEEPS + 1
ROWS = 32
SCOPED = 16 * 2**20


def pack_kernel(ph_ref, dv_ref, p_ref, vc_ref, xa_ref, xb_ref, za_ref, zb_ref, row_ref, adj_ref, up_ref, down_ref):
    cells_x = ph_ref.shape[0]
    x_even = lax.axis_index("wide") % 2 == 0
    z_even = lax.axis_index("narrow") % 2 == 0
    lane = iota(1)
    row = iota(0)
    before = None
    for i in range(cells_x):
        ph = ph_ref[i].astype(jnp.float32)
        adj = jnp.zeros_like(ph)
        if before is not None:
            adj = adj - before
        if i + 1 < cells_x:
            before = face(ph + ph_ref[i + 1].astype(jnp.float32)) * vc_ref[0, i]
            adj = adj + before
        flux = face(ph + jnp.where(row == ph.shape[0] - 1, ph, y_up(ph))) * vc_ref[1, i]
        adj = adj + flux - jnp.where(row == 0, 0.0, y_down(flux))
        flux = jnp.where(lane == ph.shape[1] - 1, 0.0, face(ph + z_up(ph)) * vc_ref[2, i])
        adj = adj + flux - z_down(flux)
        adj_ref[i] = adj

    first = cells_x - HALO
    n = SWEEPS

    def upward(out):
        out[0:HALO] = ph_ref[first:].astype(jnp.float32)
        out[HALO : HALO + n] = dv_ref[first + 1 :]
        out[HALO + n : HALO + 2 * n] = adj_ref[first + 1 :]
        out[HALO + 2 * n : HALO + 3 * n] = p_ref[first + 1 :]
        out[HALO + 3 * n] = vc_ref[0, cells_x - 1]

    def downward(out):
        out[0:HALO] = ph_ref[0:HALO].astype(jnp.float32)
        out[HALO : HALO + n] = dv_ref[0:n]
        out[HALO + n : HALO + 2 * n] = adj_ref[0:n]
        out[HALO + 2 * n : 2 * HALO + 2 * n] = p_ref[0:HALO]

    @pl.when(x_even)
    def _():
        upward(xa_ref)
        downward(xb_ref)

    @pl.when(jnp.logical_not(x_even))
    def _():
        upward(xb_ref)
        downward(xa_ref)

    cells = cells_x * ph_ref.shape[1]
    width = ph_ref.shape[2]

    def turned(v):
        return v.reshape(cells, width).T

    t = turned(ph_ref[...].astype(jnp.float32))
    up_ref[0:HALO] = t[width - HALO :]
    down_ref[0:HALO] = t[0:HALO]
    t = turned(dv_ref[...])
    up_ref[HALO : HALO + n] = t[width - n :]
    down_ref[HALO : HALO + n] = t[0:n]
    t = turned(adj_ref[...])
    up_ref[HALO + n : HALO + 2 * n] = t[width - n :]
    down_ref[HALO + n : HALO + 2 * n] = t[0:n]
    t = turned(p_ref[...])
    up_ref[HALO + 2 * n : HALO + 3 * n] = t[width - n :]
    down_ref[HALO + 2 * n : 2 * HALO + 2 * n] = t[0:HALO]
    t = turned(vc_ref[2])
    up_ref[HALO + 3 * n : HALO + 3 * n + 1] = t[width - 1 :]
    row_ref[...] = t[width - 8 :]
    t = turned(vc_ref[0])
    up_ref[2 * HALO + 2 * n + 0 : 2 * HALO + 3 * n] = t[width - n :]
    down_ref[2 * HALO + 2 * n : 2 * HALO + 3 * n] = t[0:n]

    @pl.when(z_even)
    def _():
        za_ref[...] = up_ref[...]
        zb_ref[...] = down_ref[...]

    @pl.when(jnp.logical_not(z_even))
    def _():
        zb_ref[...] = up_ref[...]
        za_ref[...] = down_ref[...]


def join_kernel(za_ref, zb_ref, edge_ref, out_ref):
    out_ref[0:ROWS] = za_ref[...]
    out_ref[ROWS : 2 * ROWS] = zb_ref[...]
    out_ref[2 * ROWS :] = edge_ref[...]


class Local:
    def __init__(self, shape, h, e, f0, c, s, ps, us, diag, vx):
        self.cells_x, self.ny, self.width = shape
        self.planes = 3 * self.cells_x
        self.h, self.e, self.f0, self.c, self.s, self.ps, self.us, self.diag, self.vx = h, e, f0, c, s, ps, us, diag, vx
        wi, ni = lax.axis_index("wide"), lax.axis_index("narrow")
        self.x_even, self.z_even = wi % 2 == 0, ni % 2 == 0
        self.x_first, self.x_last = wi == 0, wi == lax.axis_size("wide") - 1
        self.z_first, self.z_last = ni == 0, ni == lax.axis_size("narrow") - 1
        lane, self.row = iota(1), iota(0)
        self.lane0, self.lane_end = lane == 0, lane == self.width - 1
        side_high = jnp.logical_and(lane <= HALO - 1, jnp.logical_not(self.z_last))
        side_low = jnp.logical_and(lane >= self.width - HALO, jnp.logical_not(self.z_first))
        self.side = jnp.logical_or(side_low, side_high)
        self.core = jnp.logical_and(self.side, jnp.logical_or(lane < HALO - 1, lane > self.width - HALO))

    def at(self, lead, i):
        return pl.ds((lead * self.planes + i + self.cells_x) * self.ny, self.ny)

    def shifted(self, lead, i, by):
        return pl.ds((lead * self.planes + i + self.cells_x) * self.ny + by, self.ny)

    def masked(self, i, col, value, cover):
        flag = None
        if i < 0:
            flag = jnp.logical_not(self.x_first)
        elif i >= self.cells_x:
            flag = jnp.logical_not(self.x_last)
        if col == 0:
            return value if flag is None else jnp.where(flag, value, 0.0)
        return jnp.where(cover if flag is None else jnp.logical_and(cover, flag), value, 0.0)

    def halo_columns(self, part, t_ref, first):
        n, width, ny, cells_x = SWEEPS, self.width, self.ny, self.cells_x
        zl = jnp.where(self.z_even, part[ROWS : 2 * ROWS], part[0:ROWS])
        zh = jnp.where(self.z_even, part[0:ROWS], part[ROWS : 2 * ROWS])
        t_ref[0, 0:HALO] = zh[0:HALO]
        t_ref[0, width - HALO :] = zl[0:HALO]
        for field in (1, 2):
            start = HALO + (field - 1) * n
            t_ref[field, 0:n] = zh[start : start + n]
            t_ref[field, width - n :] = zl[start : start + n]
        start = HALO + 2 * n
        t_ref[3, 0:HALO] = zh[start : start + HALO]
        t_ref[3, width - n :] = zl[start : start + n]
        below = jnp.where(self.z_first, 0.0, zl[start + n : start + n + 1])
        above = part[2 * ROWS + 7 : 2 * ROWS + 8]
        t_ref[4, width - 1 :] = below
        t_ref[4, 0:1] = above
        t_ref[5, width - 1 :] = above
        t_ref[5, 0:1] = below
        for field in range(6):
            self.h[pl.ds((field * self.planes + first + cells_x) * ny, cells_x * ny)] = t_ref[field].T
        if first == cells_x:
            return
        last = slice((cells_x - 1) * ny, cells_x * ny)
        t_ref[0, 0:n, 0:ny] = zh[2 * HALO + 2 * n :, last]
        t_ref[0, width - n :, 0:ny] = zl[2 * HALO + 2 * n :, last]
        number = 0 if first < 0 else 1
        self.vx[pl.ds(number * ny, ny)] = t_ref[0, :, 0:128].T[0:ny]

    def phases(self, i, value):
        self.e[self.at(0, i)] = value
        low = jnp.logical_and(self.lane_end, self.z_first)
        high = jnp.logical_and(self.lane0, self.z_last)
        other = self.h[self.at(0, i)]
        self.e[self.at(1, i)] = jnp.where(high, z_down(value), jnp.where(low, z_up(value), other))

    def start(self, i, value):
        self.ps[self.at(0, i)] = self.masked(i, 0, value, None)
        self.ps[self.at(1, i)] = self.masked(i, 1, self.h[self.at(3, i)], self.side)

    def faces_x(self, i):
        for col in range(2):
            self.f0[self.at(col, i)] = face(self.e[self.at(col, i)] + self.e[self.at(col, i + 1)])

    def setup(self, i, source, adj, cross):
        ny, row = self.ny, self.row
        ph = [self.e[self.at(col, i)] for col in range(2)]
        up_z = [z_up(v) for v in ph]
        f2 = [face(ph[col] + jnp.where(self.lane_end, up_z[1 - col], up_z[col])) for col in range(2)]
        down_z = [z_down(v) for v in f2]
        for col in range(2):
            l2 = jnp.where(self.lane0, down_z[1 - col], down_z[col])
            up = self.e[self.shifted(col, i, 1)]
            down = self.e[self.shifted(col, i, -1)]
            f1 = face(ph[col] + jnp.where(row == ny - 1, ph[col], up))
            l1 = face(ph[col] + jnp.where(row == 0, ph[col], down))
            f0 = self.f0[self.at(col, i)]
            l0 = self.f0[self.at(col, i - 1)]
            diag = f0 + l0 + f1 + l1 + f2[col] + l2
            inv = self.masked(i, col, 1.0 / diag, self.core)
            if col == 0 and 0 <= i < self.cells_x:
                self.diag[pl.ds(i * ny, ny)] = diag
            for number, value in enumerate((f0, l0, jnp.where(row == ny - 1, 0.0, f1), jnp.where(row == 0, 0.0, l1), f2[col], l2)):
                self.c[self.at(2 * number + col, i)] = value * inv
            value = adj if col == 0 else self.h[self.at(2, i)]
            right = source if col == 0 else self.h[self.at(1, i)]
            if i in cross:
                value = value + cross[i][col]
            if i - 1 in cross:
                value = value - cross[i - 1][col]
            value = value + jnp.where(self.lane0, -l2, f2[col]) * self.h[self.at(5 - col, i)]
            if col == 1:
                value = jnp.where(self.core, value, 0.0)
                right = jnp.where(self.core, right, 0.0)
            self.s[self.at(col, i)] = right * inv
            self.us[self.at(col, i)] = value * inv

    def spread(self, state, k, i):
        v = [state[self.at(2 * k + col, i)] for col in range(2)]
        up_z = [z_up(x) for x in v]
        down_z = [z_down(x) for x in v]
        out = []
        for col in range(2):
            lead = 2 * k + col
            up = jnp.where(self.lane_end, up_z[1 - col], up_z[col])
            down = jnp.where(self.lane0, down_z[1 - col], down_z[col])
            total = self.c[self.at(col, i)] * state[self.at(lead, i + 1)] + self.c[self.at(2 + col, i)] * state[self.at(lead, i - 1)]
            total = total + self.c[self.at(4 + col, i)] * state[self.shifted(lead, i, 1)]
            total = total + self.c[self.at(6 + col, i)] * state[self.shifted(lead, i, -1)]
            out.append(total + self.c[self.at(8 + col, i)] * up + self.c[self.at(10 + col, i)] * down)
        return v, out

    def sweep_p(self, k, i):
        w = chebyshev_weights(SWEEPS)[k]
        v, total = self.spread(self.ps, k, i)
        for col in range(2):
            self.ps[self.at(2 * k + 2 + col, i)] = (1.0 - w) * v[col] + w * (self.s[self.at(col, i)] + total[col])

    def sweep_u(self, k, i):
        w = chebyshev_weights(SWEEPS)[SWEEPS - 1 - k]
        v, total = self.spread(self.us, k, i)
        for col in range(2):
            self.us[self.at(2 * k + 2 + col, i)] = (1.0 - w) * v[col] + w * total[col]


def early(k, cells_x):
    return range(1 + k, cells_x - 1 - k), range(2 + k, cells_x - 2 - k)


def own_kernel(
    ph_ref, dv_ref, p_ref, adj_ref, own_ref,
    h_ref, e_ref, f0_ref, c_ref, s_ref, ps_ref, us_ref, diag_ref, vx_ref, t_ref,
):
    g = Local(ph_ref.shape, h_ref, e_ref, f0_ref, c_ref, s_ref, ps_ref, us_ref, diag_ref, vx_ref)
    cells_x = g.cells_x
    t_ref[...] = jnp.zeros_like(t_ref)
    g.halo_columns(own_ref[...], t_ref, 0)
    for i in range(cells_x):
        g.phases(i, ph_ref[i].astype(jnp.float32))
        g.start(i, p_ref[i])
    zero = jnp.zeros((g.ny, g.width), jnp.float32)
    for col in range(2):
        for i in (-1, cells_x):
            e_ref[g.at(col, i)] = zero
            for k in range(SWEEPS):
                for state in (ps_ref, us_ref):
                    state[g.at(2 * k + col, i)] = zero
        for k in range(SWEEPS):
            for i in range(cells_x):
                if k > 0 and i not in early(k - 1, cells_x)[0]:
                    ps_ref[g.at(2 * k + col, i)] = zero
                us_ref[g.at(2 * k + col, i)] = zero
    for i in range(cells_x - 1):
        g.faces_x(i)
    for i in range(1, cells_x - 1):
        g.setup(i, dv_ref[i], adj_ref[i], {})
    for k in range(SWEEPS):
        for_p, for_u = early(k, cells_x)
        for i in for_p:
            g.sweep_p(k, i)
        for i in for_u:
            g.sweep_u(k, i)


def main_kernel(
    ph_ref, dv_ref, p_ref, vc_ref, adj_ref, xa_ref, xb_ref, ca_ref, cb_ref,
    h_in, e_in, f0_in, c_in, s_in, ps_in, us_in, diag_in, vx_in,
    h_ref, e_ref, f0_ref, c_ref, s_ref, ps_ref, us_ref, diag_ref, vx_ref, gd_ref, gp_ref, gf_ref,
    t_ref, r_ref,
):
    g = Local(ph_ref.shape, h_ref, e_ref, f0_ref, c_ref, s_ref, ps_ref, us_ref, diag_ref, vx_ref)
    cells_x, ny, width, row = g.cells_x, g.ny, g.width, g.row
    n = SWEEPS
    weights = chebyshev_weights(SWEEPS)
    lane_end = g.lane_end

    def low(k):
        return jnp.where(g.x_even, xb_ref[k], xa_ref[k])

    def high(k):
        return jnp.where(g.x_even, xa_ref[k], xb_ref[k])

    t_ref[...] = jnp.zeros_like(t_ref)
    g.halo_columns(jnp.where(g.x_even, cb_ref[...], ca_ref[...]), t_ref.at[0], -cells_x)
    g.halo_columns(jnp.where(g.x_even, ca_ref[...], cb_ref[...]), t_ref.at[1], cells_x)
    for k in range(HALO):
        g.phases(k - HALO, low(k))
        g.phases(cells_x + k, high(k))
    for col in range(2):
        e_ref[g.at(col, -1)] = jnp.where(g.x_first, e_ref[g.at(col, 0)], e_ref[g.at(col, -1)])
        end = e_ref[g.at(col, cells_x - 1)]
        e_ref[g.at(col, cells_x)] = jnp.where(g.x_last, end, e_ref[g.at(col, cells_x)])
    for i in range(-n, 0):
        g.start(i, low(HALO + 3 * n + i))
    for i in range(cells_x, cells_x + HALO):
        g.start(i, high(HALO + 2 * n + i - cells_x))
    for i in (*range(-HALO, 0), *range(cells_x - 1, cells_x + n)):
        g.faces_x(i)

    cross = {}
    for number, i in enumerate((-1, cells_x - 1)):
        value = low(HALO + 3 * n) if i < 0 else vc_ref[0, i]
        flux = (f0_ref[g.at(0, i)] * value, f0_ref[g.at(1, i)] * vx_ref[pl.ds(number * ny, ny)])
        cross[i] = tuple(jnp.where(g.x_first, 0.0, v) for v in flux) if i < 0 else flux

    zero = jnp.zeros((ny, width), jnp.float32)
    for col in range(2):
        for i in (-n - 1, cells_x + n):
            us_ref[g.at(col, i)] = zero
    for i in (*range(-n, 1), *range(cells_x - 1, cells_x + n)):
        if i < 0:
            g.setup(i, low(HALO + n + i), low(HALO + 2 * n + i), cross)
        elif i >= cells_x:
            g.setup(i, high(HALO + i - cells_x), high(HALO + n + i - cells_x), cross)
        else:
            g.setup(i, dv_ref[i], adj_ref[i], cross)

    for k in range(n):
        for_p, for_u = early(k, cells_x)
        for i in range(-(n - 1) + k, cells_x + n - k):
            if i not in for_p:
                g.sweep_p(k, i)
            if i not in for_u and i < cells_x + n - 1 - k:
                g.sweep_u(k, i)

    for i in range(cells_x + 1):
        for col in range(2):
            total = None
            for k in range(n):
                term = us_ref[g.at(2 * (n - 1 - k) + col, i)] * (ps_ref[g.at(2 * k + 2 + col, i)] - ps_ref[g.at(2 * k + col, i)])
                total = term if total is None else total + term
            r_ref[g.at(col, i)] = total

    def rises(state, k, i):
        v = state[g.at(2 * k, i)]
        z_next = jnp.where(lane_end, z_up(state[g.at(2 * k + 1, i)]), z_up(v))
        y_next = jnp.where(row == ny - 1, 0.0, state[g.shifted(2 * k, i, 1)])
        return v, (state[g.at(2 * k, i + 1)] - v, y_next - v, z_next - v)

    for i in range(cells_x):
        gp_ref[i] = us_ref[g.at(2 * n, i)] * diag_ref[pl.ds(i * ny, ny)]
        gd = zero
        terms = [zero] * 3
        for k in range(n):
            u, rise_u = rises(us_ref, n - 1 - k, i)
            _, rise_p = rises(ps_ref, k, i)
            gd = gd + weights[k] * u
            for a in range(3):
                terms[a] = terms[a] + weights[k] * (rise_u[a] * rise_p[a])
        gd_ref[i] = gd
        _, rise = rises(ps_ref, n, i)
        r = r_ref[g.at(0, i)]
        y_next = jnp.where(row == ny - 1, 0.0, r_ref[g.shifted(0, i, 1)])
        z_next = jnp.where(lane_end, z_up(r_ref[g.at(1, i)]), z_up(r))
        nexts = (r_ref[g.at(0, i + 1)], y_next, z_next)
        for a in range(3):
            gf_ref[a, i] = -vc_ref[a, i] * rise[a] - terms[a] - (r + nexts[a])


def swaps(size, other, odd, spare_first):
    pairs = []
    for i in range(size):
        for k in range(other):
            partner = ((i + 1) ^ 1) - 1 if odd else i ^ 1
            target = (partner, k) if 0 <= partner < size else (i, k ^ 1)
            source = (i, k)
            pairs.append((source, target))
    return pairs


def flat_pairs(pairs, narrow, turned):
    def flat(at):
        return at[1] * narrow + at[0] if turned else at[0] * narrow + at[1]

    return [(flat(source), flat(target)) for source, target in pairs]


def per_device(divergence, pressure_start, phase, velocity_cot):
    cells_x, ny, cells_z = divergence.shape
    wide, narrow = lax.axis_size("wide"), lax.axis_size("narrow")
    axes = ("wide", "narrow")
    x_even = flat_pairs(swaps(wide, narrow, False, True), narrow, False)
    x_odd = flat_pairs(swaps(wide, narrow, True, True), narrow, False)
    z_even = flat_pairs(swaps(narrow, wide, False, True), narrow, True)
    z_odd = flat_pairs(swaps(narrow, wide, True, True), narrow, True)
    f32 = jnp.float32
    vmem = pl.BlockSpec(memory_space=pltpu.VMEM)

    def kept(*dims):
        return pltpu.VMEM(dims, f32)

    def near(v):
        return pltpu.with_memory_space_constraint(v, pltpu.VMEM)

    slots = 2 * HALO + 2 * SWEEPS
    cells = cells_x * ny
    phase, divergence, pressure_start, velocity_cot = (
        near(v) for v in (phase, divergence, pressure_start, velocity_cot)
    )
    xa, xb, za, zb, edge, adj = pl.pallas_call(
        pack_kernel,
        out_shape=(
            kept(slots, ny, cells_z), kept(slots, ny, cells_z), kept(ROWS, cells), kept(ROWS, cells),
            kept(8, cells), kept(cells_x, ny, cells_z),
        ),
        in_specs=[vmem] * 4,
        out_specs=(vmem,) * 6,
        scratch_shapes=[pltpu.VMEM((ROWS, cells), f32)] * 2,
        compiler_params=pltpu.CompilerParams(vmem_limit_bytes=SCOPED),
        name="pack",
    )(phase, divergence, pressure_start, velocity_cot)

    got_xb = near(lax.ppermute(xb, axes, x_odd))
    got_xa = near(lax.ppermute(xa, axes, x_even))
    got_za = near(lax.ppermute(za, axes, z_even))
    got_zb = near(lax.ppermute(zb, axes, z_odd))
    corner = pl.pallas_call(
        join_kernel,
        out_shape=kept(2 * ROWS + 8, cells),
        in_specs=[vmem] * 3,
        out_specs=vmem,
        compiler_params=pltpu.CompilerParams(vmem_limit_bytes=SCOPED),
        name="join",
    )(got_za, got_zb, edge)
    got_cb = near(lax.ppermute(corner, axes, x_odd))
    got_ca = near(lax.ppermute(corner, axes, x_even))

    rows = 3 * cells_x * ny
    layers = (6, 2, 2, 12, 2, 2 * (SWEEPS + 1), 2 * (SWEEPS + 1))
    shapes = (*(kept(layer * rows, cells_z) for layer in layers), kept(cells_x * ny, cells_z), kept(2 * ny, cells_z))
    state = pl.pallas_call(
        own_kernel,
        out_shape=shapes,
        in_specs=[vmem] * 5,
        out_specs=(vmem,) * len(shapes),
        scratch_shapes=[pltpu.VMEM((6, cells_z, cells), f32)],
        compiler_params=pltpu.CompilerParams(vmem_limit_bytes=SCOPED),
        name="own",
    )(phase, divergence, pressure_start, adj, corner)

    block = jax.ShapeDtypeStruct((cells_x, ny, cells_z), f32)
    out = pl.pallas_call(
        main_kernel,
        out_shape=(*shapes, block, block, jax.ShapeDtypeStruct((3, cells_x, ny, cells_z), f32)),
        in_specs=[vmem] * (9 + len(shapes)),
        out_specs=(vmem,) * (len(shapes) + 3),
        input_output_aliases={9 + number: number for number in range(len(shapes))},
        scratch_shapes=[pltpu.VMEM((2, 6, cells_z, cells), f32), pltpu.VMEM((2 * rows, cells_z), f32)],
        compiler_params=pltpu.CompilerParams(vmem_limit_bytes=SCOPED),
        name="sweeps",
    )(phase, divergence, pressure_start, velocity_cot, adj, got_xa, got_xb, got_ca, got_cb, *state)
    return out[-3:]


def solution(mesh):
    in_specs = (
        P("wide", None, "narrow"),
        P("wide", None, "narrow"),
        P("wide", None, "narrow"),
        P(None, "wide", None, "narrow"),
    )
    out_specs = (
        P("wide", None, "narrow"),
        P("wide", None, "narrow"),
        P(None, "wide", None, "narrow"),
    )
    return jax.shard_map(
        per_device, mesh=mesh, in_specs=in_specs, out_specs=out_specs, check_vma=False
    )
```
